512 devices in a mesh: seq: 64 (over z, x), head: 8 (over y, core).
Axes of the slice: x: 4, y: 4, z: 16, core: 2. Of those that a mesh axis runs over, the one named last changes fastest.
Arguments:
- tokens: bfloat16 [65536, 1024], P('seq'), may hold values from -60 to 60
- qkv_weight: bfloat16 [1024, 8, 384], P(None, 'head'), may hold values from -0.1875 to 0.1875
- out_weight: bfloat16 [8, 128, 1024], P('head'), may hold values from -0.1875 to 0.1875
- members: int32 [8, 256, 768], P('head', None, 'seq'), may hold values from 0 to 65535, as said below
- counts: int32 [8, 64, 256], P('head', 'seq'), may hold values from 1 to 12, as said below
Outputs:
- mixed: bfloat16 [65536, 1024], P(('seq', 'head'))
- centroids: float32 [8, 256, 128], P('head', 'seq')
The draws below stay inside these ranges and needn't reach their ends.
Inputs may be any that keep to these rules, and one draw needn't show every extreme that they name: `members`: the entries of slots j of any cluster lie in slab j // 12, i.e. in positions 1024 * (j // 12) up to 1024 * (j // 12 + 1) - 1. For each head and slab, the valid entries (j % 12 < counts) over all clusters name every token of that slab exactly once; the other entries are padding with some position of the same slab. For each head and slab the counts over the 256 clusters sum to 1024. For each head, one cluster has 12 members from every slab. Split the 256 clusters into 64 aligned groups of equal size; for each head and slab the counts of one group sum to at most 32, and exactly 32 for the group that holds the full cluster.
All inputs are finite; a program needn't handle non-finite values.
Results may differ from the reference program's by a relative error of at most 0.02.
The reference program's roundings to bfloat16 on the way (of `projected`, `probs`, `attended` and `head_out`) count: a program that leaves them out, or rounds other values in their place, can miss the bound.
Values may be sent and summed in bfloat16 or wider, within the bound.
A program may use at most 128 MiB of HBM per device.

```python
import jax
import jax.numpy as jnp
from jax import lax

D = 1024
H = 8
HD = 128
K = 256
S_C = 12
TOK_DEV = 1024
TOKENS = 65536
W = 768
N_SEQ = 64


def cluster_plan(key):
    base = jax.random.fold_in(key, 11)
    owned = K // N_SEQ
    limit = min(owned * S_C, max(owned + S_C - 1, 2 * TOK_DEV // N_SEQ))
    extra = K * (S_C - 1)

    def one_slab(head_key, full, slab):
        slab_key = jax.random.fold_in(head_key, slab)
        key_rank, key_perm, key_fill = jax.random.split(slab_key, 3)
        extra_ids = jnp.arange(extra, dtype=jnp.int32)
        cluster_of = extra_ids // (S_C - 1)
        owner_of = cluster_of // owned
        ranks = jax.random.permutation(key_rank, extra).astype(jnp.int32)
        inner_key = owner_of * (extra + 1) + jnp.where(cluster_of == full, -1, ranks) + 1
        inner_order = jnp.argsort(inner_key, stable=True).astype(jnp.int32)
        inner_rank = jnp.zeros((extra,), jnp.int32).at[inner_order].set(extra_ids)
        in_owner = inner_rank - owner_of * (owned * (S_C - 1))
        eligible = in_owner < limit - owned
        full_owner = full // owned
        outer_key = jnp.where(eligible, jnp.where(owner_of == full_owner, -1, ranks), extra)
        order = jnp.argsort(outer_key, stable=True).astype(jnp.int32)
        placed = jnp.zeros((extra,), jnp.int32).at[order].set(extra_ids)
        chosen = (placed < TOK_DEV - K).astype(jnp.int32)
        slab_counts = 1 + jnp.sum(chosen.reshape(K, S_C - 1), axis=1)
        offsets = jnp.cumsum(slab_counts) - slab_counts
        shuffled = jax.random.permutation(key_perm, TOK_DEV).astype(jnp.int32) + slab * TOK_DEV
        slot_ids = jnp.arange(S_C, dtype=jnp.int32)
        index = jnp.minimum(offsets[:, None] + slot_ids[None, :], TOK_DEV - 1)
        filler = jax.random.randint(key_fill, (K, S_C), 0, TOK_DEV, dtype=jnp.int32) + slab * TOK_DEV
        member_ids = jnp.where(slot_ids[None, :] < slab_counts[:, None], shuffled[index], filler)
        return (member_ids, slab_counts)

    def one_head(head):
        head_key = jax.random.fold_in(base, head)
        full = jax.random.randint(jax.random.fold_in(head_key, 99991), (), 0, K, dtype=jnp.int32)
        return jax.vmap(lambda slab: one_slab(head_key, full, slab))(jnp.arange(N_SEQ, dtype=jnp.int32))
    member_ids, slab_counts = jax.vmap(one_head)(jnp.arange(H, dtype=jnp.int32))
    member_ids = jnp.transpose(member_ids, (0, 2, 1, 3)).reshape(H, K, N_SEQ * S_C)
    return (member_ids, slab_counts)


def draw_members(key, part):
    return cluster_plan(key)[0]


def draw_counts(key, part):
    return cluster_plan(key)[1]


def draw_tokens(key, part):
    key_main = jax.random.fold_in(jax.random.fold_in(key, 5), 0)
    values = jnp.clip(jax.random.normal(key_main, (TOKENS, D), jnp.float32), -6.0, 6.0)
    return values.astype(jnp.bfloat16)


def levels(stream_key, extent, cuts, least, high):
    factor_of = 1.0
    for position, blocks in cuts:
        draws = jax.random.uniform(jax.random.fold_in(jax.random.fold_in(stream_key, 6), position), (blocks,), jnp.float32, least / len(cuts), high / len(cuts))
        factor_of = factor_of * jnp.repeat(jnp.exp(draws), extent[position] // blocks).reshape((-1,) + (1,) * (len(extent) - 1 - position))
    return factor_of


def bell_draw(rng, dims, spread, bound, pieces=(), held_as=jnp.bfloat16):
    result = spread * jax.random.normal(rng, dims, jnp.float32)
    if pieces:
        result = result * levels(rng, dims, pieces, -0.22, 0.18)
    return jnp.clip(result, -bound, bound).astype(held_as)


def setup_inputs(seed: int = 0) -> dict:
    streams_of = jax.random.split(jax.random.key(seed), 6)
    return {
        "tokens": draw_tokens(jax.random.fold_in(streams_of[5], 71), 0),
        "qkv_weight": bell_draw(streams_of[1], (D, H, 3 * HD), D ** -0.5, 0.1875, ((1, 8),)),
        "out_weight": bell_draw(streams_of[2], (H, HD, D), (H * HD) ** -0.5, 0.1875, ((0, 8),)),
        "members": draw_members(jax.random.fold_in(streams_of[5], 71), 0),
        "counts": draw_counts(jax.random.fold_in(streams_of[5], 71), 0),
    }


eps_norm = 1e-06

def reference(tokens, qkv_weight, out_weight, members, counts):
    slot_ids = jnp.arange(W, dtype=jnp.int32)
    slab_of = slot_ids // S_C
    within = slot_ids % S_C
    scale = 1.0 / HD ** 0.5

    def one_head(carry, inputs):
        weight_qkv, weight_out, member_ids, slab_counts = inputs
        projected = jnp.dot(tokens, weight_qkv, preferred_element_type=jnp.float32).astype(jnp.bfloat16)
        keys_all = projected[:, HD:2 * HD].astype(jnp.float32)
        unit_keys = keys_all * lax.rsqrt(lax.optimization_barrier(jnp.sum(keys_all * keys_all, axis=1, keepdims=True)) + eps_norm)
        valid = within[None, :] < slab_counts[slab_of, :].T
        positions = jnp.where(valid, member_ids, -1)
        gathered = unit_keys[member_ids]
        cluster_sums = lax.optimization_barrier(jnp.sum(jnp.where(valid[:, :, None], gathered, 0.0), axis=1))
        centroid = cluster_sums * lax.rsqrt(lax.optimization_barrier(jnp.mean(cluster_sums * cluster_sums, axis=1, keepdims=True)) + eps_norm)

        def cluster(args):
            member_row, position_row = args
            member_data = projected[member_row]
            queries = member_data[:, :HD]
            keys_in = member_data[:, HD:2 * HD]
            values_in = member_data[:, 2 * HD:]
            scores = jnp.dot(queries, keys_in.T, preferred_element_type=jnp.float32) * scale
            allowed = (position_row[None, :] >= 0) & (position_row[None, :] <= position_row[:, None]) | jnp.eye(W, dtype=bool)
            masked = jnp.where(allowed, scores, -1e+30)
            highest = lax.optimization_barrier(jnp.max(masked, axis=1, keepdims=True))
            expo = jnp.exp(masked - highest)
            probs = (expo / lax.optimization_barrier(jnp.sum(expo, axis=1, keepdims=True))).astype(jnp.bfloat16)
            return jnp.dot(probs, values_in, preferred_element_type=jnp.float32).astype(jnp.bfloat16)
        attended = lax.map(cluster, (member_ids, positions))
        target = jnp.where(positions >= 0, member_ids, TOKENS).astype(jnp.int32)
        head_out = jnp.zeros((TOKENS, HD), jnp.bfloat16).at[target.reshape(-1)].set(attended.reshape(-1, HD), mode='drop')
        carry = carry + jnp.dot(head_out, weight_out, preferred_element_type=jnp.float32)
        return (carry, centroid)
    start = jnp.zeros((TOKENS, D), jnp.float32)
    total, centroids = lax.scan(one_head, start, (jnp.transpose(qkv_weight, (1, 0, 2)), out_weight, members, counts))
    return (total.astype(jnp.bfloat16), centroids)
```

```python
import functools

import jax
import jax.numpy as jnp
from jax import lax
from jax.experimental import pallas as pl
from jax.experimental.pallas import tpu as pltpu
from jax.sharding import PartitionSpec as P

MESH = pl.DeviceIdType.MESH
eps_norm = 1e-06
f32, bf16, i32 = jnp.float32, jnp.bfloat16, jnp.int32


def iota(shape, dim):
    return lax.broadcasted_iota(i32, shape, dim)


def nt_dot(a, b):
    return lax.dot_general(a, b, (((1,), (1,)), ((), ())), preferred_element_type=f32)


def layer_kernel(
    nx, batch, q_rows,
    tokens, wqkv, wo, slot_ids, cnt,
    mixed, cent,
    proj, pick, put, qk_s, v_s, qk_r, v_r, probs, o_s, o_r, acc, hs, hr, wo_r,
    cnt_s, tab_r, tab, held, cl_col,
    send_sem, cnt_sem, qk_sem, v_sem, o_sem, h_sem, wo_sem,
):
    n, heads = lax.axis_size("seq"), lax.axis_size("head")
    me, my_head = lax.axis_index("seq"), lax.axis_index("head")
    nz = n // nx
    my_z, my_x = me // nx, lax.rem(me, nx)
    slab, hd = proj.shape[0], wo.shape[0]
    cap = qk_s.shape[0] // n
    clusters = cnt.shape[1]
    owned = clusters // n
    s_c = slot_ids.shape[0]
    batches = n // batch
    rows_b = batch * cap
    out_rows = mixed.shape[0]

    def peer(step):
        dz = lax.rem((step // nx) * 7, nz)
        return lax.rem(my_z + dz, nz) * nx + lax.rem(my_x + lax.rem(step, nx), nx)

    def block(ref, index, size):
        return ref.at[pl.ds(pl.multiple_of(index * size, size), size), :]

    def remote(src, dst, ssem, rsem, where):
        return pltpu.make_async_remote_copy(
            src_ref=src, dst_ref=dst, send_sem=ssem, recv_sem=rsem,
            device_id=where, device_id_type=MESH,
        )

    barrier = pltpu.get_barrier_semaphore()

    @pl.loop(1, n)
    def _(step):
        pl.semaphore_signal(barrier, inc=1, device_id={"seq": peer(step)}, device_id_type=MESH)

    @pl.loop(1, heads)
    def _(step):
        pl.semaphore_signal(
            barrier, inc=1, device_id={"head": lax.rem(my_head + step, heads)}, device_id_type=MESH
        )

    local = slot_ids[...] - me * slab
    count = cnt[...]
    rank = jnp.zeros((s_c, clusters), i32)
    for j in range(s_c):
        rank += jnp.where((local[j : j + 1, :] < local) & (count > j), 1, 0)
    wide = jnp.broadcast_to(count, (8, clusters))
    lane4 = lax.rem(iota((8, clusters), 1), owned)
    start = jnp.zeros((8, clusters), i32)
    for k in range(1, owned):
        start += jnp.where(lane4 >= k, pltpu.roll(wide, k, 1), 0)
    slot = jnp.where(iota((s_c, clusters), 0) < count, rank + start[:1, :], -1)
    token = jnp.zeros((cap, clusters), f32)
    row = iota((cap, clusters), 0)
    for j in range(s_c):
        token += jnp.where(slot[j : j + 1, :] == row, (local[j : j + 1, :] + 1).astype(f32), 0.0)
    total = token
    for k in range(1, owned):
        total += pltpu.roll(token, clusters - k, 1)
    held[...] = total
    cnt_s[...] = count.astype(f32)

    proj[...] = jnp.dot(tokens[...], wqkv[...], preferred_element_type=f32).astype(bf16)

    pl.semaphore_wait(barrier, n - 1 + heads - 1)

    @pl.loop(1, n)
    def _(step):
        remote(cnt_s, tab_r.at[me], send_sem.at[0], cnt_sem, {"seq": peer(step)}).start()

    pltpu.make_async_copy(cnt_s, tab_r.at[me], cnt_sem).start()

    def send_qk(step):
        remote(block(qk_s, step, cap), block(qk_r, me, cap), send_sem.at[1], qk_sem,
               {"seq": peer(step)}).start()

    def send_v(step):
        remote(block(v_s, step, cap), block(v_r, me, cap), send_sem.at[2], v_sem,
               {"seq": peer(step)}).start()

    col = iota((cap, slab), 1)
    lane = iota((cap, clusters), 1)

    @pl.loop(0, batches)
    def _(b):
        @pl.loop(0, batch)
        def _(i):
            step = b * batch + i
            mine = jnp.sum(
                jnp.where(lane == owned * peer(step), held[...], 0.0), axis=1, keepdims=True
            )
            hit = jnp.where((col + 1).astype(f32) == mine, 1.0, 0.0)
            pick[pl.ds(pl.multiple_of(step * cap, cap), cap), :] = hit.astype(bf16)

        at = pl.ds(pl.multiple_of(b * rows_b, rows_b), rows_b)
        rows = jnp.dot(pick[at, :], proj[...], preferred_element_type=f32).astype(bf16)
        qk_s[at, :] = rows[:, : 2 * hd]
        v_s[at, :] = rows[:, 2 * hd :]

        @pl.loop(0, batch)
        def _(i):
            step = b * batch + i

            @pl.when(step > 0)
            def _():
                send_qk(step)

    pltpu.make_async_copy(block(qk_s, 0, cap), block(qk_r, me, cap), qk_sem).start()

    @pl.loop(1, n)
    def _(step):
        send_v(step)

    pltpu.make_async_copy(block(v_s, 0, cap), block(v_r, me, cap), v_sem).start()

    @pl.loop(1, heads)
    def _(step):
        remote(wo, block(wo_r, my_head, hd), send_sem.at[3], wo_sem,
               {"head": lax.rem(my_head + step, heads)}).start()

    pltpu.make_async_copy(wo, block(wo_r, my_head, hd), wo_sem).start()

    for b in range(batches):
        part = pick[b * rows_b : (b + 1) * rows_b, :].astype(f32)
        put[:, b * rows_b : (b + 1) * rows_b] = part.T.astype(bf16)

    pltpu.make_async_copy(tab_r, tab_r, cnt_sem).wait()

    @pl.loop(0, n)
    def _(s):
        tab[pl.ds(s, 1), :] = tab_r[s]

    table = tab[...].astype(bf16)

    def ends(rows_k):
        k_id, c_id = iota((rows_k, clusters), 0), iota((rows_k, clusters), 1)
        inside = (c_id // owned == me) & (lax.rem(c_id, owned) <= k_id)
        return jnp.where(inside, 1.0, 0.0).astype(bf16)

    total_rows = n * cap
    spread_t = jnp.where(iota((n, total_rows), 1) // cap == iota((n, total_rows), 0), 1.0, 0.0)
    end_row = jnp.dot(
        nt_dot(ends(8), table).astype(bf16), spread_t.astype(bf16), preferred_element_type=f32
    )
    past = (lax.rem(iota((8, total_rows), 1), cap).astype(f32) >= end_row) & (
        iota((8, total_rows), 0) < owned
    )
    cl_row = jnp.sum(jnp.where(past, 1.0, 0.0), axis=0, keepdims=True)
    spread = jnp.where(iota((total_rows, n), 0) // cap == iota((total_rows, n), 1), 1.0, 0.0)
    end_col = jnp.dot(
        spread.astype(bf16), nt_dot(table, ends(128)).astype(bf16), preferred_element_type=f32
    )
    past = (lax.rem(iota((total_rows, 128), 0), cap).astype(f32) >= end_col) & (
        iota((total_rows, 128), 1) < owned
    )
    cl_col[...] = jnp.sum(jnp.where(past, 1.0, 0.0), axis=1, keepdims=True)

    pltpu.make_async_copy(qk_r, qk_r, qk_sem).wait()
    scale = hd ** (-0.5)

    @pl.loop(0, total_rows // q_rows)
    def _(c):
        at = pl.ds(pl.multiple_of(c * q_rows, q_rows), q_rows)
        scores = nt_dot(qk_r[at, :hd], qk_r[:, hd:]) * scale
        ahead = iota((q_rows, total_rows), 1) <= iota((q_rows, total_rows), 0) + c * q_rows
        allowed = (cl_col[at, :] == cl_row) & ahead
        masked = jnp.where(allowed, scores, -1e30)
        expo = jnp.exp(masked - jnp.max(masked, axis=1, keepdims=True))
        probs[at, :] = (expo / jnp.sum(expo, axis=1, keepdims=True)).astype(bf16)

    sums = [jnp.zeros((1, hd), f32) for _ in range(owned)]
    keys = qk_r[:, hd:].astype(f32)
    unit = keys * lax.rsqrt(jnp.sum(keys * keys, axis=1, keepdims=True) + eps_norm)
    for k in range(owned):
        kept = jnp.where(cl_col[...] == float(k), unit, 0.0)
        one = jnp.sum(kept, axis=0, keepdims=True)
        cent[k : k + 1, :] = one * lax.rsqrt(jnp.mean(one * one, axis=1, keepdims=True) + eps_norm)

    pltpu.make_async_copy(v_r, v_r, v_sem).wait()

    @pl.loop(0, batches)
    def _(b):
        turn = lax.rem(my_z * nx // batch + 3 * b, batches)
        at = pl.ds(pl.multiple_of(turn * rows_b, rows_b), rows_b)
        o_s[at, :] = jnp.dot(probs[at, :], v_r[...], preferred_element_type=f32).astype(bf16)

        @pl.loop(0, batch)
        def _(i):
            s = turn * batch + i
            step = (
                lax.rem(7 * lax.rem(my_z - s // nx + nz, nz), nz) * nx
                + lax.rem(my_x - lax.rem(s, nx) + nx, nx)
            )

            @pl.when(s != me)
            def _():
                remote(block(o_s, s, cap), block(o_r, step, cap), send_sem.at[4],
                       o_sem.at[step // batch], {"seq": s}).start()

            @pl.when(s == me)
            def _():
                pltpu.make_async_copy(
                    block(o_s, s, cap), block(o_r, step, cap), o_sem.at[step // batch]
                ).start()

    acc[...] = jnp.zeros_like(acc)
    for b in range(batches):
        at = pl.ds(b * rows_b, rows_b)
        pltpu.make_async_copy(o_r.at[at, :], o_r.at[at, :], o_sem.at[b]).wait()
        acc[...] += jnp.dot(put[:, b * rows_b : (b + 1) * rows_b], o_r[at, :],
                            preferred_element_type=f32)
    hs[...] = acc[...].astype(bf16)

    @pl.loop(1, heads)
    def _(step):
        to = lax.rem(my_head + step, heads)
        remote(block(hs, to, out_rows), hr.at[my_head], send_sem.at[5], h_sem,
               {"head": to}).start()

    pltpu.make_async_copy(block(hs, my_head, out_rows), hr.at[my_head], h_sem).start()
    pltpu.make_async_copy(wo_r, wo_r, wo_sem).wait()
    pltpu.make_async_copy(hr, hr, h_sem).wait()
    all_heads = jnp.concatenate([hr[h] for h in range(heads)], axis=1)
    mixed[...] = jnp.dot(all_heads, wo_r[...], preferred_element_type=f32).astype(bf16)

    def sent(ref, index):
        pltpu.make_async_copy(ref, ref, send_sem.at[index]).wait()

    sent(tab_r.at[pl.ds(0, n - 1)], 0)
    sent(qk_s.at[pl.ds(0, (n - 1) * cap), :], 1)
    sent(v_s.at[pl.ds(0, (n - 1) * cap), :], 2)
    sent(wo_r.at[pl.ds(0, (heads - 1) * hd), :], 3)
    sent(o_s.at[pl.ds(0, (n - 1) * cap), :], 4)
    sent(hr.at[pl.ds(0, heads - 1)], 5)


def on_device(nx, tokens, qkv_weight, out_weight, members, counts):
    slab, width = tokens.shape
    heads, n = lax.axis_size("head"), lax.axis_size("seq")
    hd = out_weight.shape[1]
    clusters, s_c = members.shape[1], members.shape[2]
    cap = 2 * slab // n
    rows = n * cap
    batch = min(8, n // 2)
    vm = lambda shape, dtype: pltpu.VMEM(shape, dtype)
    mixed, centroids = pl.pallas_call(
        functools.partial(layer_kernel, nx, batch, 128),
        out_shape=(
            jax.ShapeDtypeStruct((slab // heads, width), bf16),
            jax.ShapeDtypeStruct((clusters // n, hd), f32),
        ),
        in_specs=[pl.BlockSpec(memory_space=pltpu.VMEM)] * 5,
        out_specs=(pl.BlockSpec(memory_space=pltpu.VMEM),) * 2,
        scratch_shapes=[
            vm((slab, 3 * hd), bf16),
            vm((rows, slab), bf16),
            vm((slab, rows), bf16),
            vm((rows, 2 * hd), bf16),
            vm((rows, hd), bf16),
            vm((rows, 2 * hd), bf16),
            vm((rows, hd), bf16),
            vm((rows, rows), bf16),
            vm((rows, hd), bf16),
            vm((rows, hd), bf16),
            vm((slab, hd), f32),
            vm((slab, hd), bf16),
            vm((heads, slab // heads, hd), bf16),
            vm((heads * hd, width), bf16),
            vm((1, clusters), f32),
            vm((n, 1, clusters), f32),
            vm((n, clusters), f32),
            vm((cap, clusters), f32),
            vm((rows, 1), f32),
            pltpu.SemaphoreType.DMA((6,)),
            pltpu.SemaphoreType.DMA,
            pltpu.SemaphoreType.DMA,
            pltpu.SemaphoreType.DMA,
            pltpu.SemaphoreType.DMA((n // batch,)),
            pltpu.SemaphoreType.DMA,
            pltpu.SemaphoreType.DMA,
        ],
        compiler_params=pltpu.CompilerParams(
            collective_id=0, has_side_effects=True, vmem_limit_bytes=56 << 20
        ),
    )(
        tokens,
        qkv_weight.reshape(width, 3 * hd),
        out_weight.reshape(hd, width),
        members.reshape(clusters, s_c).T,
        counts.reshape(1, clusters),
    )
    return mixed, centroids[None]


def solution(mesh):
    n = mesh.shape["seq"]
    return jax.shard_map(
        functools.partial(on_device, min(4, n // 4)),
        mesh=mesh,
        in_specs=(
            P("seq", None),
            P(None, "head", None),
            P("head", None, None),
            P("head", None, "seq"),
            P("head", "seq", None),
        ),
        out_specs=(P(("seq", "head"), None), P("head", "seq", None)),
        check_vma=False,
    )
```

```python
import functools

import jax
import jax.numpy as jnp
from jax import lax
from jax.experimental import pallas as pl
from jax.experimental.pallas import tpu as pltpu
from jax.sharding import PartitionSpec as P

MESH = pl.DeviceIdType.MESH
eps_norm = 1e-06
f32, bf16, i32 = jnp.float32, jnp.bfloat16, jnp.int32


def iota(shape, dim):
    return lax.broadcasted_iota(i32, shape, dim)


def nt_dot(a, b):
    return lax.dot_general(a, b, (((1,), (1,)), ((), ())), preferred_element_type=f32)


def layer_kernel(
    nx, batch, q_rows,
    tokens_hbm, wqkv_hbm, wo, ids_hbm, cnt_hbm,
    all_heads, all_wo, cent,
    tokens, wqkv, ids, cnt, proj, pick, put, qk_s, v_s, qk_r, v_r, probs, o_s, o_r, acc, hs,
    cnt_s, tab_r, tab, held, cl_col,
    in_sem, send_sem, cnt_sem, qk_sem, v_sem, o_sem, h_sem, wo_sem,
):
    n, heads = lax.axis_size("seq"), lax.axis_size("head")
    me, my_head = lax.axis_index("seq"), lax.axis_index("head")
    nz = n // nx
    my_z, my_x = me // nx, lax.rem(me, nx)
    slab, hd = proj.shape[0], wo.shape[0]
    cap = qk_s.shape[0] // n
    clusters = cnt.shape[1]
    pairs = nz // 2
    my_pair, my_odd = my_z // 2, lax.rem(my_z, 2)
    owned = clusters // n
    s_c = ids.shape[0]
    batches = n // batch
    rows_b = batch * cap
    out_rows = all_heads.shape[0]

    def offset(b):
        return pairs // 2 + (b + 1) // 2 * (1 - 2 * lax.rem(b, 2))

    own_step = (batches - 1) * batch

    def peer(step):
        b, i = step // batch, lax.rem(step, batch)
        pair = lax.rem(my_pair + offset(b), pairs)
        return (pair * 2 + lax.rem(my_odd + i // nx, 2)) * nx + lax.rem(my_x + i, nx)

    def block(ref, index, size):
        return ref.at[pl.ds(pl.multiple_of(index * size, size), size), :]

    def remote(src, dst, ssem, rsem, where):
        return pltpu.make_async_remote_copy(
            src_ref=src, dst_ref=dst, send_sem=ssem, recv_sem=rsem,
            device_id=where, device_id_type=MESH,
        )

    loads = [
        pltpu.make_async_copy(ids_hbm, ids, in_sem.at[0]),
        pltpu.make_async_copy(cnt_hbm, cnt, in_sem.at[1]),
        pltpu.make_async_copy(wqkv_hbm, wqkv, in_sem.at[2]),
        pltpu.make_async_copy(tokens_hbm, tokens, in_sem.at[3]),
    ]
    for load in loads:
        load.start()

    barrier = pltpu.get_barrier_semaphore()

    @pl.loop(1, n)
    def _(step):
        pl.semaphore_signal(
            barrier, inc=1, device_id={"seq": lax.rem(me + step, n)}, device_id_type=MESH
        )

    @pl.loop(1, heads)
    def _(step):
        pl.semaphore_signal(
            barrier, inc=1, device_id={"head": lax.rem(my_head + step, heads)}, device_id_type=MESH
        )

    loads[0].wait()
    loads[1].wait()
    local = jnp.concatenate([ids[j] for j in range(s_c)], axis=0) - me * slab
    count = cnt[...]
    rank = jnp.zeros((s_c, clusters), i32)
    for j in range(s_c):
        rank += jnp.where((local[j : j + 1, :] < local) & (count > j), 1, 0)
    wide = jnp.broadcast_to(count, (8, clusters))
    lane4 = lax.rem(iota((8, clusters), 1), owned)
    start = jnp.zeros((8, clusters), i32)
    for k in range(1, owned):
        start += jnp.where(lane4 >= k, pltpu.roll(wide, k, 1), 0)
    slot = jnp.where(iota((s_c, clusters), 0) < count, rank + start[:1, :], -1)
    token = jnp.zeros((cap, clusters), f32)
    row = iota((cap, clusters), 0)
    for j in range(s_c):
        token += jnp.where(slot[j : j + 1, :] == row, (local[j : j + 1, :] + 1).astype(f32), 0.0)
    total = token
    for k in range(1, owned):
        total += pltpu.roll(token, clusters - k, 1)
    held[...] = total
    cnt_s[...] = count.astype(f32)

    col = (iota((cap, slab), 1) + 1).astype(f32)
    lane = iota((cap, clusters), 1)

    def gather_batch(b):
        for i in range(batch):
            step = b * batch + i
            mine = jnp.sum(
                jnp.where(lane == owned * peer(step), held[...], 0.0), axis=1, keepdims=True
            )
            hit = jnp.where(col == mine, 1.0, 0.0)
            pick[pl.ds(pl.multiple_of(step * cap, cap), cap), :] = hit.astype(bf16)

        at = pl.ds(pl.multiple_of(b * rows_b, rows_b), rows_b)
        rows = jnp.dot(pick[at, :], proj[...], preferred_element_type=f32).astype(bf16)
        qk_s[at, :] = rows[:, : 2 * hd]
        v_s[at, :] = rows[:, 2 * hd :]

    def send_qk(step):
        remote(block(qk_s, step, cap), block(qk_r, me, cap), send_sem.at[1], qk_sem,
               {"seq": peer(step)}).start()

    def send_v(step):
        remote(block(v_s, step, cap), block(v_r, me, cap), send_sem.at[2], v_sem,
               {"seq": peer(step)}).start()

    loads[2].wait()
    loads[3].wait()
    proj[...] = jnp.dot(tokens[...], wqkv[...], preferred_element_type=f32).astype(bf16)
    gather_batch(0)

    pl.semaphore_wait(barrier, n - 1 + heads - 1)

    @pl.loop(1, nz)
    def _(dz):
        remote(cnt_s, tab_r.at[my_x, my_z], send_sem.at[0], cnt_sem.at[0],
               {"seq": lax.rem(my_z + dz, nz) * nx + my_x}).start()

    pltpu.make_async_copy(cnt_s, tab_r.at[my_x, my_z], cnt_sem.at[0]).start()

    @pl.loop(0, batch)
    def _(step):
        send_qk(step)

    @pl.loop(1, batches - 1)
    def _(b):
        gather_batch(b)

        @pl.loop(0, batch)
        def _(i):
            send_qk(b * batch + i)

    gather_batch(batches - 1)

    @pl.loop(own_step + 1, n)
    def _(step):
        send_qk(step)

    pltpu.make_async_copy(block(qk_s, own_step, cap), block(qk_r, me, cap), qk_sem).start()

    column = tab_r.at[my_x]
    pltpu.make_async_copy(column, column, cnt_sem.at[0]).wait()

    @pl.loop(1, nx)
    def _(dx):
        remote(column, column, send_sem.at[6], cnt_sem.at[1],
               {"seq": my_z * nx + lax.rem(my_x + dx, nx)}).start()

    @pl.loop(0, own_step)
    def _(step):
        send_v(step)

    @pl.loop(own_step + 1, n)
    def _(step):
        send_v(step)

    pltpu.make_async_copy(block(v_s, own_step, cap), block(v_r, me, cap), v_sem).start()

    @pl.loop(1, heads)
    def _(step):
        remote(wo, block(all_wo, my_head, hd), send_sem.at[3], wo_sem,
               {"head": lax.rem(my_head + step, heads)}).start()

    pltpu.make_async_copy(wo, block(all_wo, my_head, hd), wo_sem).start()

    for b in range(batches):
        part = pick[b * rows_b : (b + 1) * rows_b, :].astype(f32)
        put[:, b * rows_b : (b + 1) * rows_b] = part.T.astype(bf16)

    others = tab_r.at[pl.ds(0, nx - 1)]
    pltpu.make_async_copy(others, others, cnt_sem.at[1]).wait()

    @pl.loop(0, n)
    def _(s):
        tab[pl.ds(s, 1), :] = tab_r[lax.rem(s, nx), s // nx]

    table = tab[...].astype(bf16)

    def ends(rows_k):
        k_id, c_id = iota((rows_k, clusters), 0), iota((rows_k, clusters), 1)
        inside = (c_id // owned == me) & (lax.rem(c_id, owned) <= k_id)
        return jnp.where(inside, 1.0, 0.0).astype(bf16)

    total_rows = n * cap
    spread_t = jnp.where(iota((n, total_rows), 1) // cap == iota((n, total_rows), 0), 1.0, 0.0)
    end_row = jnp.dot(
        nt_dot(ends(8), table).astype(bf16), spread_t.astype(bf16), preferred_element_type=f32
    )
    past = (lax.rem(iota((8, total_rows), 1), cap).astype(f32) >= end_row) & (
        iota((8, total_rows), 0) < owned
    )
    cl_row = jnp.sum(jnp.where(past, 1.0, 0.0), axis=0, keepdims=True)
    spread = jnp.where(iota((total_rows, n), 0) // cap == iota((total_rows, n), 1), 1.0, 0.0)
    end_col = jnp.dot(
        spread.astype(bf16), nt_dot(table, ends(128)).astype(bf16), preferred_element_type=f32
    )
    past = (lax.rem(iota((total_rows, 128), 0), cap).astype(f32) >= end_col) & (
        iota((total_rows, 128), 1) < owned
    )
    cl_col[...] = jnp.sum(jnp.where(past, 1.0, 0.0), axis=1, keepdims=True)

    pltpu.make_async_copy(qk_r, qk_r, qk_sem).wait()
    scale = hd ** (-0.5)

    @pl.loop(0, total_rows // q_rows)
    def _(c):
        at = pl.ds(pl.multiple_of(c * q_rows, q_rows), q_rows)
        scores = nt_dot(qk_r[at, :hd], qk_r[:, hd:]) * scale
        ahead = iota((q_rows, total_rows), 1) <= iota((q_rows, total_rows), 0) + c * q_rows
        allowed = (cl_col[at, :] == cl_row) & ahead
        masked = jnp.where(allowed, scores, -1e30)
        expo = jnp.exp(masked - jnp.max(masked, axis=1, keepdims=True))
        probs[at, :] = (expo / jnp.sum(expo, axis=1, keepdims=True)).astype(bf16)

    sums = [jnp.zeros((1, hd), f32) for _ in range(owned)]
    keys = qk_r[:, hd:].astype(f32)
    unit = keys * lax.rsqrt(jnp.sum(keys * keys, axis=1, keepdims=True) + eps_norm)
    for k in range(owned):
        kept = jnp.where(cl_col[...] == float(k), unit, 0.0)
        one = jnp.sum(kept, axis=0, keepdims=True)
        cent[k : k + 1, :] = one * lax.rsqrt(jnp.mean(one * one, axis=1, keepdims=True) + eps_norm)

    pltpu.make_async_copy(v_r, v_r, v_sem).wait()

    @pl.loop(0, batches)
    def _(b):
        turn = lax.rem(my_pair + 2 * pairs - offset(b), pairs)
        at = pl.ds(pl.multiple_of(turn * rows_b, rows_b), rows_b)
        o_s[at, :] = jnp.dot(probs[at, :], v_r[...], preferred_element_type=f32).astype(bf16)

        @pl.loop(0, batch)
        def _(i):
            s = turn * batch + i
            step = (
                b * batch
                + lax.rem(my_z + s // nx, 2) * nx
                + lax.rem(my_x - lax.rem(s, nx) + nx, nx)
            )

            @pl.when(s != me)
            def _():
                remote(block(o_s, s, cap), block(o_r, step, cap), send_sem.at[4],
                       o_sem.at[b], {"seq": s}).start()

            @pl.when(s == me)
            def _():
                pltpu.make_async_copy(
                    block(o_s, s, cap), block(o_r, step, cap), o_sem.at[b]
                ).start()

    acc[...] = jnp.zeros_like(acc)
    for b in range(batches):
        at = pl.ds(b * rows_b, rows_b)
        pltpu.make_async_copy(o_r.at[at, :], o_r.at[at, :], o_sem.at[b]).wait()
        acc[...] += jnp.dot(put[:, b * rows_b : (b + 1) * rows_b], o_r[at, :],
                            preferred_element_type=f32)
    hs[...] = acc[...].astype(bf16)
    lanes = all_heads.at[:, pl.ds(pl.multiple_of(my_head * hd, hd), hd)]

    @pl.loop(1, heads)
    def _(step):
        to = lax.rem(my_head + step, heads)
        remote(block(hs, to, out_rows), lanes, send_sem.at[5], h_sem, {"head": to}).start()

    pltpu.make_async_copy(block(hs, my_head, out_rows), lanes, h_sem).start()
    pltpu.make_async_copy(all_wo, all_wo, wo_sem).wait()
    pltpu.make_async_copy(all_heads, all_heads, h_sem).wait()

    def sent(ref, index):
        pltpu.make_async_copy(ref, ref, send_sem.at[index]).wait()

    sent(tab_r.at[0, pl.ds(0, nz - 1)], 0)
    sent(others, 6)
    sent(qk_s.at[pl.ds(0, (n - 1) * cap), :], 1)
    sent(v_s.at[pl.ds(0, (n - 1) * cap), :], 2)
    sent(all_wo.at[pl.ds(0, (heads - 1) * hd), :], 3)
    sent(o_s.at[pl.ds(0, (n - 1) * cap), :], 4)
    sent(hs.at[pl.ds(0, (heads - 1) * out_rows), :], 5)


def mix_kernel(all_heads, all_wo, cent_in, mixed, cent):
    mixed[...] = jnp.dot(all_heads[...], all_wo[...], preferred_element_type=f32).astype(bf16)
    cent[...] = cent_in[...]


def on_device(nx, tokens, qkv_weight, out_weight, members, counts):
    slab, width = tokens.shape
    heads, n = lax.axis_size("head"), lax.axis_size("seq")
    hd = out_weight.shape[1]
    clusters, s_c = members.shape[1], members.shape[2]
    cap = 2 * slab // n
    rows = n * cap
    batch = 2 * nx
    vm = lambda shape, dtype: pltpu.VMEM(shape, dtype)
    all_heads, all_wo, centroids = pl.pallas_call(
        functools.partial(layer_kernel, nx, batch, 128),
        out_shape=(
            jax.ShapeDtypeStruct((slab // heads, heads * hd), bf16),
            jax.ShapeDtypeStruct((heads * hd, width), bf16),
            jax.ShapeDtypeStruct((clusters // n, hd), f32),
        ),
        in_specs=[pl.BlockSpec(memory_space=pltpu.HBM)] * 5,
        out_specs=(
            pl.BlockSpec(memory_space=pltpu.HBM),
            pl.BlockSpec(memory_space=pltpu.HBM),
            pl.BlockSpec(memory_space=pltpu.VMEM),
        ),
        scratch_shapes=[
            vm((slab, width), bf16),
            vm((width, 3 * hd), bf16),
            vm((s_c, 1, clusters), i32),
            vm((1, clusters), i32),
            vm((slab, 3 * hd), bf16),
            vm((rows, slab), bf16),
            vm((slab, rows), bf16),
            vm((rows, 2 * hd), bf16),
            vm((rows, hd), bf16),
            vm((rows, 2 * hd), bf16),
            vm((rows, hd), bf16),
            vm((rows, rows), bf16),
            vm((rows, hd), bf16),
            vm((rows, hd), bf16),
            vm((slab, hd), f32),
            vm((slab, hd), bf16),
            vm((1, clusters), f32),
            vm((nx, n // nx, 1, clusters), f32),
            vm((n, clusters), f32),
            vm((cap, clusters), f32),
            vm((rows, 1), f32),
            pltpu.SemaphoreType.DMA((4,)),
            pltpu.SemaphoreType.DMA((7,)),
            pltpu.SemaphoreType.DMA((2,)),
            pltpu.SemaphoreType.DMA,
            pltpu.SemaphoreType.DMA,
            pltpu.SemaphoreType.DMA((n // batch,)),
            pltpu.SemaphoreType.DMA,
            pltpu.SemaphoreType.DMA,
        ],
        compiler_params=pltpu.CompilerParams(
            collective_id=0, has_side_effects=True, vmem_limit_bytes=56 << 20
        ),
    )(
        tokens,
        qkv_weight.reshape(width, 3 * hd),
        out_weight.reshape(hd, width),
        jnp.transpose(members, (2, 0, 1)),
        counts.reshape(1, clusters),
    )
    steps = 4
    block = width // steps
    mixed, centroids = pl.pallas_call(
        mix_kernel,
        grid=(steps,),
        out_shape=(
            jax.ShapeDtypeStruct((slab // heads, width), bf16),
            jax.ShapeDtypeStruct(centroids.shape, f32),
        ),
        in_specs=[
            pl.BlockSpec(all_heads.shape, lambda i: (0, 0)),
            pl.BlockSpec((heads * hd, block), lambda i: (0, i)),
            pl.BlockSpec(centroids.shape, lambda i: (0, 0)),
        ],
        out_specs=(
            pl.BlockSpec((slab // heads, block), lambda i: (0, i)),
            pl.BlockSpec(centroids.shape, lambda i: (0, 0)),
        ),
    )(all_heads, all_wo, centroids)
    return mixed, centroids[None]


def solution(mesh):
    n = mesh.shape["seq"]
    return jax.shard_map(
        functools.partial(on_device, min(4, n // 4)),
        mesh=mesh,
        in_specs=(
            P("seq", None),
            P(None, "head", None),
            P("head", None, None),
            P("head", None, "seq"),
            P("head", "seq", None),
        ),
        out_specs=(P(("seq", "head"), None), P("head", "seq", None)),
        check_vma=False,
    )
```

```python
import functools

import jax
import jax.numpy as jnp
from jax import lax
from jax.experimental import pallas as pl
from jax.experimental.pallas import tpu as pltpu
from jax.sharding import PartitionSpec as P

MESH = pl.DeviceIdType.MESH
eps_norm = 1e-06
f32, bf16, i32 = jnp.float32, jnp.bfloat16, jnp.int32


def iota(shape, dim):
    return lax.broadcasted_iota(i32, shape, dim)


def nt_dot(a, b):
    return lax.dot_general(a, b, (((1,), (1,)), ((), ())), preferred_element_type=f32)


def layer_kernel(
    nx, batch, q_rows,
    tokens_hbm, wqkv_hbm, wo, ids_hbm, cnt_hbm,
    all_heads, all_wo, cent,
    tokens, wqkv, ids, cnt, proj, pick, put, qk_s, v_s, qk_r, v_r, probs, o_s, o_r, acc, hs,
    cnt_s, tab_r, tab, held, cl_col,
    in_sem, send_sem, cnt_sem, qk_sem, v_sem, o_sem, h_sem, wo_sem,
):
    n, heads = lax.axis_size("seq"), lax.axis_size("head")
    me, my_head = lax.axis_index("seq"), lax.axis_index("head")
    nz = n // nx
    my_z, my_x = me // nx, lax.rem(me, nx)
    slab, hd = proj.shape[0], wo.shape[0]
    cap = qk_s.shape[0] // n
    clusters = cnt.shape[1]
    pairs = nz // 2
    my_pair, my_odd = my_z // 2, lax.rem(my_z, 2)
    owned = clusters // n
    s_c = ids.shape[0]
    batches = n // batch
    rows_b = batch * cap
    out_rows = all_heads.shape[0]

    def offset(b):
        return pairs // 2 + (b + 1) // 2 * (1 - 2 * lax.rem(b, 2))

    own_step = (batches - 1) * batch

    def peer(step):
        b, i = step // batch, lax.rem(step, batch)
        pair = lax.rem(my_pair + offset(b), pairs)
        return (pair * 2 + lax.rem(my_odd + i // nx, 2)) * nx + lax.rem(my_x + i, nx)

    def block(ref, index, size):
        return ref.at[pl.ds(pl.multiple_of(index * size, size), size), :]

    def remote(src, dst, ssem, rsem, where):
        return pltpu.make_async_remote_copy(
            src_ref=src, dst_ref=dst, send_sem=ssem, recv_sem=rsem,
            device_id=where, device_id_type=MESH,
        )

    loads = [
        pltpu.make_async_copy(ids_hbm, ids, in_sem.at[0]),
        pltpu.make_async_copy(cnt_hbm, cnt, in_sem.at[1]),
        pltpu.make_async_copy(wqkv_hbm, wqkv, in_sem.at[2]),
        pltpu.make_async_copy(tokens_hbm, tokens, in_sem.at[3]),
    ]
    for load in loads:
        load.start()

    barrier = pltpu.get_barrier_semaphore()

    @pl.loop(1, n)
    def _(step):
        pl.semaphore_signal(
            barrier, inc=1, device_id={"seq": lax.rem(me + step, n)}, device_id_type=MESH
        )

    @pl.loop(1, heads)
    def _(step):
        pl.semaphore_signal(
            barrier, inc=1, device_id={"head": lax.rem(my_head + step, heads)}, device_id_type=MESH
        )

    loads[0].wait()
    loads[1].wait()
    local = jnp.concatenate([ids[j] for j in range(s_c)], axis=0) - me * slab
    count = cnt[...]
    rank = jnp.zeros((s_c, clusters), i32)
    for j in range(s_c):
        rank += jnp.where((local[j : j + 1, :] < local) & (count > j), 1, 0)
    wide = jnp.broadcast_to(count, (8, clusters))
    lane4 = lax.rem(iota((8, clusters), 1), owned)
    start = jnp.zeros((8, clusters), i32)
    for k in range(1, owned):
        start += jnp.where(lane4 >= k, pltpu.roll(wide, k, 1), 0)
    slot = jnp.where(iota((s_c, clusters), 0) < count, rank + start[:1, :], -1)
    token = jnp.zeros((cap, clusters), f32)
    row = iota((cap, clusters), 0)
    for j in range(s_c):
        token += jnp.where(slot[j : j + 1, :] == row, (local[j : j + 1, :] + 1).astype(f32), 0.0)
    total = token
    for k in range(1, owned):
        total += pltpu.roll(token, clusters - k, 1)
    held[...] = total
    cnt_s[...] = count.astype(f32)

    col = (iota((cap, slab), 1) + 1).astype(f32)
    lane = iota((cap, clusters), 1)

    def gather_batch(b):
        for i in range(batch):
            step = b * batch + i
            mine = jnp.sum(
                jnp.where(lane == owned * peer(step), held[...], 0.0), axis=1, keepdims=True
            )
            hit = jnp.where(col == mine, 1.0, 0.0)
            pick[pl.ds(pl.multiple_of(step * cap, cap), cap), :] = hit.astype(bf16)

        at = pl.ds(pl.multiple_of(b * rows_b, rows_b), rows_b)
        rows = jnp.dot(pick[at, :], proj[...], preferred_element_type=f32).astype(bf16)
        qk_s[at, :] = rows[:, : 2 * hd]
        v_s[at, :] = rows[:, 2 * hd :]

    def send_qk(step):
        remote(block(qk_s, step, cap), block(qk_r, me, cap), send_sem.at[1], qk_sem,
               {"seq": peer(step)}).start()

    def send_v(step):
        remote(block(v_s, step, cap), block(v_r, me, cap), send_sem.at[2], v_sem,
               {"seq": peer(step)}).start()

    loads[2].wait()
    loads[3].wait()
    proj[...] = jnp.dot(tokens[...], wqkv[...], preferred_element_type=f32).astype(bf16)
    gather_batch(0)

    pl.semaphore_wait(barrier, n - 1 + heads - 1)

    @pl.loop(1, nz)
    def _(dz):
        remote(cnt_s, tab_r.at[my_x, my_z], send_sem.at[0], cnt_sem.at[0],
               {"seq": lax.rem(my_z + dz, nz) * nx + my_x}).start()

    pltpu.make_async_copy(cnt_s, tab_r.at[my_x, my_z], cnt_sem.at[0]).start()

    @pl.loop(0, batch)
    def _(step):
        send_qk(step)

    @pl.loop(1, batches - 1)
    def _(b):
        gather_batch(b)

        @pl.loop(0, batch)
        def _(i):
            send_qk(b * batch + i)

    gather_batch(batches - 1)

    @pl.loop(own_step + 1, n)
    def _(step):
        send_qk(step)

    pltpu.make_async_copy(block(qk_s, own_step, cap), block(qk_r, me, cap), qk_sem).start()

    column = tab_r.at[my_x]
    pltpu.make_async_copy(column, column, cnt_sem.at[0]).wait()

    @pl.loop(1, nx)
    def _(dx):
        remote(column, column, send_sem.at[6], cnt_sem.at[1],
               {"seq": my_z * nx + lax.rem(my_x + dx, nx)}).start()

    @pl.loop(0, own_step)
    def _(step):
        send_v(step)

    @pl.loop(own_step + 1, n)
    def _(step):
        send_v(step)

    pltpu.make_async_copy(block(v_s, own_step, cap), block(v_r, me, cap), v_sem).start()

    @pl.loop(1, heads)
    def _(step):
        remote(wo, block(all_wo, my_head, hd), send_sem.at[3], wo_sem,
               {"head": lax.rem(my_head + step, heads)}).start()

    pltpu.make_async_copy(wo, block(all_wo, my_head, hd), wo_sem).start()

    for b in range(batches):
        part = pick[b * rows_b : (b + 1) * rows_b, :].astype(f32)
        put[:, b * rows_b : (b + 1) * rows_b] = part.T.astype(bf16)

    others = tab_r.at[pl.ds(0, nx - 1)]
    pltpu.make_async_copy(others, others, cnt_sem.at[1]).wait()

    @pl.loop(0, n)
    def _(s):
        tab[pl.ds(s, 1), :] = tab_r[lax.rem(s, nx), s // nx]

    table = tab[...].astype(bf16)

    def ends(rows_k):
        k_id, c_id = iota((rows_k, clusters), 0), iota((rows_k, clusters), 1)
        inside = (c_id // owned == me) & (lax.rem(c_id, owned) <= k_id)
        return jnp.where(inside, 1.0, 0.0).astype(bf16)

    total_rows = n * cap
    spread_t = jnp.where(iota((n, total_rows), 1) // cap == iota((n, total_rows), 0), 1.0, 0.0)
    end_row = jnp.dot(
        nt_dot(ends(8), table).astype(bf16), spread_t.astype(bf16), preferred_element_type=f32
    )
    past = (lax.rem(iota((8, total_rows), 1), cap).astype(f32) >= end_row) & (
        iota((8, total_rows), 0) < owned
    )
    cl_row = jnp.sum(jnp.where(past, 1.0, 0.0), axis=0, keepdims=True)
    spread = jnp.where(iota((total_rows, n), 0) // cap == iota((total_rows, n), 1), 1.0, 0.0)
    end_col = jnp.dot(
        spread.astype(bf16), nt_dot(table, ends(128)).astype(bf16), preferred_element_type=f32
    )
    past = (lax.rem(iota((total_rows, 128), 0), cap).astype(f32) >= end_col) & (
        iota((total_rows, 128), 1) < owned
    )
    cl_col[...] = jnp.sum(jnp.where(past, 1.0, 0.0), axis=1, keepdims=True)

    pltpu.make_async_copy(qk_r, qk_r, qk_sem).wait()
    scale = hd ** (-0.5)

    @pl.loop(0, total_rows // q_rows)
    def _(c):
        at = pl.ds(pl.multiple_of(c * q_rows, q_rows), q_rows)
        scores = nt_dot(qk_r[at, :hd], qk_r[:, hd:]) * scale
        ahead = iota((q_rows, total_rows), 1) <= iota((q_rows, total_rows), 0) + c * q_rows
        allowed = (cl_col[at, :] == cl_row) & ahead
        masked = jnp.where(allowed, scores, -1e30)
        expo = jnp.exp(masked - jnp.max(masked, axis=1, keepdims=True))
        probs[at, :] = (expo / jnp.sum(expo, axis=1, keepdims=True)).astype(bf16)

    sums = [jnp.zeros((1, hd), f32) for _ in range(owned)]
    keys = qk_r[:, hd:].astype(f32)
    unit = keys * lax.rsqrt(jnp.sum(keys * keys, axis=1, keepdims=True) + eps_norm)
    for k in range(owned):
        kept = jnp.where(cl_col[...] == float(k), unit, 0.0)
        one = jnp.sum(kept, axis=0, keepdims=True)
        cent[k : k + 1, :] = one * lax.rsqrt(jnp.mean(one * one, axis=1, keepdims=True) + eps_norm)

    pltpu.make_async_copy(v_r, v_r, v_sem).wait()

    @pl.loop(0, batches)
    def _(b):
        turn = lax.rem(my_pair + 2 * pairs - offset(b), pairs)
        at = pl.ds(pl.multiple_of(turn * rows_b, rows_b), rows_b)
        o_s[at, :] = jnp.dot(probs[at, :], v_r[...], preferred_element_type=f32).astype(bf16)

        @pl.loop(0, batch)
        def _(i):
            s = turn * batch + i
            step = (
                b * batch
                + lax.rem(my_z + s // nx, 2) * nx
                + lax.rem(my_x - lax.rem(s, nx) + nx, nx)
            )

            @pl.when(s != me)
            def _():
                remote(block(o_s, s, cap), block(o_r, step, cap), send_sem.at[4],
                       o_sem.at[b], {"seq": s}).start()

            @pl.when(s == me)
            def _():
                pltpu.make_async_copy(
                    block(o_s, s, cap), block(o_r, step, cap), o_sem.at[b]
                ).start()

    acc[...] = jnp.zeros_like(acc)
    for b in range(batches):
        at = pl.ds(b * rows_b, rows_b)
        pltpu.make_async_copy(o_r.at[at, :], o_r.at[at, :], o_sem.at[b]).wait()
        acc[...] += jnp.dot(put[:, b * rows_b : (b + 1) * rows_b], o_r[at, :],
                            preferred_element_type=f32)
    hs[...] = acc[...].astype(bf16)
    lanes = all_heads.at[:, pl.ds(pl.multiple_of(my_head * hd, hd), hd)]

    @pl.loop(1, heads)
    def _(step):
        to = lax.rem(my_head + step, heads)
        remote(block(hs, to, out_rows), lanes, send_sem.at[5], h_sem, {"head": to}).start()

    pltpu.make_async_copy(block(hs, my_head, out_rows), lanes, h_sem).start()
    pltpu.make_async_copy(all_wo, all_wo, wo_sem).wait()
    pltpu.make_async_copy(all_heads, all_heads, h_sem).wait()

    def sent(ref, index):
        pltpu.make_async_copy(ref, ref, send_sem.at[index]).wait()

    sent(tab_r.at[0, pl.ds(0, nz - 1)], 0)
    sent(others, 6)
    sent(qk_s.at[pl.ds(0, (n - 1) * cap), :], 1)
    sent(v_s.at[pl.ds(0, (n - 1) * cap), :], 2)
    sent(all_wo.at[pl.ds(0, (heads - 1) * hd), :], 3)
    sent(o_s.at[pl.ds(0, (n - 1) * cap), :], 4)
    sent(hs.at[pl.ds(0, (heads - 1) * out_rows), :], 5)


def mix_kernel(all_heads, all_wo, cent_in, mixed_hbm, cent_hbm, mixed, sems):
    parts = sems.shape[0] - 1
    size = mixed.shape[1] // parts
    copies = [pltpu.make_async_copy(cent_in, cent_hbm, sems.at[parts])]
    copies[0].start()
    for c in range(parts):
        at = pl.ds(c * size, size)
        mixed[:, at] = jnp.dot(
            all_heads[...], all_wo[:, at], preferred_element_type=f32
        ).astype(bf16)
        copies.append(pltpu.make_async_copy(mixed.at[:, at], mixed_hbm.at[:, at], sems.at[c]))
        copies[-1].start()
    for copy in copies:
        copy.wait()


def on_device(nx, tokens, qkv_weight, out_weight, members, counts):
    slab, width = tokens.shape
    heads, n = lax.axis_size("head"), lax.axis_size("seq")
    hd = out_weight.shape[1]
    clusters, s_c = members.shape[1], members.shape[2]
    cap = 2 * slab // n
    rows = n * cap
    batch = 2 * nx
    vm = lambda shape, dtype: pltpu.VMEM(shape, dtype)
    all_heads, all_wo, centroids = pl.pallas_call(
        functools.partial(layer_kernel, nx, batch, 128),
        out_shape=(
            vm((slab // heads, heads * hd), bf16),
            vm((heads * hd, width), bf16),
            vm((clusters // n, hd), f32),
        ),
        in_specs=[pl.BlockSpec(memory_space=pltpu.HBM)] * 5,
        out_specs=(
            pl.BlockSpec(memory_space=pltpu.VMEM),
            pl.BlockSpec(memory_space=pltpu.VMEM),
            pl.BlockSpec(memory_space=pltpu.VMEM),
        ),
        scratch_shapes=[
            vm((slab, width), bf16),
            vm((width, 3 * hd), bf16),
            vm((s_c, 1, clusters), i32),
            vm((1, clusters), i32),
            vm((slab, 3 * hd), bf16),
            vm((rows, slab), bf16),
            vm((slab, rows), bf16),
            vm((rows, 2 * hd), bf16),
            vm((rows, hd), bf16),
            vm((rows, 2 * hd), bf16),
            vm((rows, hd), bf16),
            vm((rows, rows), bf16),
            vm((rows, hd), bf16),
            vm((rows, hd), bf16),
            vm((slab, hd), f32),
            vm((slab, hd), bf16),
            vm((1, clusters), f32),
            vm((nx, n // nx, 1, clusters), f32),
            vm((n, clusters), f32),
            vm((cap, clusters), f32),
            vm((rows, 1), f32),
            pltpu.SemaphoreType.DMA((4,)),
            pltpu.SemaphoreType.DMA((7,)),
            pltpu.SemaphoreType.DMA((2,)),
            pltpu.SemaphoreType.DMA,
            pltpu.SemaphoreType.DMA,
            pltpu.SemaphoreType.DMA((n // batch,)),
            pltpu.SemaphoreType.DMA,
            pltpu.SemaphoreType.DMA,
        ],
        compiler_params=pltpu.CompilerParams(
            collective_id=0, has_side_effects=True, vmem_limit_bytes=44 << 20
        ),
    )(
        *(
            pltpu.with_memory_space_constraint(x, pltpu.HBM)
            for x in (
                tokens,
                qkv_weight.reshape(width, 3 * hd),
                out_weight.reshape(hd, width),
                jnp.transpose(members, (2, 0, 1)),
                counts.reshape(1, clusters),
            )
        )
    )
    parts = 2
    mixed, centroids = pl.pallas_call(
        mix_kernel,
        out_shape=(
            jax.ShapeDtypeStruct((slab // heads, width), bf16),
            jax.ShapeDtypeStruct(centroids.shape, f32),
        ),
        in_specs=[pl.BlockSpec(memory_space=pltpu.VMEM)] * 3,
        out_specs=(pl.BlockSpec(memory_space=pltpu.HBM),) * 2,
        scratch_shapes=[
            vm((slab // heads, width), bf16),
            pltpu.SemaphoreType.DMA((parts + 1,)),
        ],
    )(*(pltpu.with_memory_space_constraint(x, pltpu.VMEM) for x in (all_heads, all_wo, centroids)))
    return mixed, centroids[None]


def solution(mesh):
    n = mesh.shape["seq"]
    return jax.shard_map(
        functools.partial(on_device, min(4, n // 4)),
        mesh=mesh,
        in_specs=(
            P("seq", None),
            P(None, "head", None),
            P("head", None, None),
            P("head", None, "seq"),
            P("head", "seq", None),
        ),
        out_specs=(P(("seq", "head"), None), P("head", "seq", None)),
        check_vma=False,
    )
```

```python
import functools

import jax
import jax.numpy as jnp
from jax import lax
from jax.experimental import pallas as pl
from jax.experimental.pallas import tpu as pltpu
from jax.sharding import PartitionSpec as P

MESH = pl.DeviceIdType.MESH
eps_norm = 1e-06
f32, bf16, i32 = jnp.float32, jnp.bfloat16, jnp.int32


def iota(shape, dim):
    return lax.broadcasted_iota(i32, shape, dim)


def nt_dot(a, b):
    return lax.dot_general(a, b, (((1,), (1,)), ((), ())), preferred_element_type=f32)


def layer_kernel(
    nx, batch, q_rows,
    tokens_hbm, wqkv_hbm, wo, ids_hbm, cnt_hbm,
    all_heads, all_wo, cent,
    tokens, wqkv, ids, cnt, proj, pick, put, qk_s, v_s, qk_r, v_r, probs, o_s, o_r, acc, hs,
    cnt_s, tab_r, tab, held, cl_col,
    in_sem, send_sem, cnt_sem, qk_sem, v_sem, o_sem, h_sem, wo_sem,
):
    n, heads = lax.axis_size("seq"), lax.axis_size("head")
    me, my_head = lax.axis_index("seq"), lax.axis_index("head")
    nz = n // nx
    my_z, my_x = me // nx, lax.rem(me, nx)
    slab, hd = proj.shape[0], wo.shape[0]
    cap = qk_s.shape[0] // n
    clusters = cnt.shape[1]
    pairs = nz // 2
    my_pair, my_odd = my_z // 2, lax.rem(my_z, 2)
    owned = clusters // n
    s_c = ids.shape[0]
    batches = n // batch
    rows_b = batch * cap
    out_rows = all_heads.shape[0]

    def offset(b):
        return pairs // 2 + (b + 1) // 2 * (1 - 2 * lax.rem(b, 2))

    own_step = (batches - 1) * batch

    def peer(step):
        b, i = step // batch, lax.rem(step, batch)
        pair = lax.rem(my_pair + offset(b), pairs)
        return (pair * 2 + lax.rem(my_odd + i // nx, 2)) * nx + lax.rem(my_x + i, nx)

    def block(ref, index, size):
        return ref.at[pl.ds(pl.multiple_of(index * size, size), size), :]

    def remote(src, dst, ssem, rsem, where):
        return pltpu.make_async_remote_copy(
            src_ref=src, dst_ref=dst, send_sem=ssem, recv_sem=rsem,
            device_id=where, device_id_type=MESH,
        )

    loads = [
        pltpu.make_async_copy(ids_hbm, ids, in_sem.at[0]),
        pltpu.make_async_copy(cnt_hbm, cnt, in_sem.at[1]),
        pltpu.make_async_copy(wqkv_hbm, wqkv, in_sem.at[2]),
        pltpu.make_async_copy(tokens_hbm, tokens, in_sem.at[3]),
    ]
    for load in loads:
        load.start()

    barrier = pltpu.get_barrier_semaphore()

    @pl.loop(1, n)
    def _(step):
        pl.semaphore_signal(
            barrier, inc=1, device_id={"seq": lax.rem(me + step, n)}, device_id_type=MESH
        )

    @pl.loop(1, heads)
    def _(step):
        pl.semaphore_signal(
            barrier, inc=1, device_id={"head": lax.rem(my_head + step, heads)}, device_id_type=MESH
        )

    loads[0].wait()
    loads[1].wait()
    local = jnp.concatenate([ids[j] for j in range(s_c)], axis=0) - me * slab
    count = cnt[...]
    rank = jnp.zeros((s_c, clusters), i32)
    for j in range(s_c):
        rank += jnp.where((local[j : j + 1, :] < local) & (count > j), 1, 0)
    wide = jnp.broadcast_to(count, (8, clusters))
    lane4 = lax.rem(iota((8, clusters), 1), owned)
    start = jnp.zeros((8, clusters), i32)
    for k in range(1, owned):
        start += jnp.where(lane4 >= k, pltpu.roll(wide, k, 1), 0)
    slot = jnp.where(iota((s_c, clusters), 0) < count, rank + start[:1, :], -1)
    token = jnp.zeros((cap, clusters), f32)
    row = iota((cap, clusters), 0)
    for j in range(s_c):
        token += jnp.where(slot[j : j + 1, :] == row, (local[j : j + 1, :] + 1).astype(f32), 0.0)
    total = token
    for k in range(1, owned):
        total += pltpu.roll(token, clusters - k, 1)
    held[...] = total
    cnt_s[...] = count.astype(f32)

    col = (iota((cap, slab), 1) + 1).astype(f32)
    lane = iota((cap, clusters), 1)

    def gather_batch(b):
        for i in range(batch):
            step = b * batch + i
            mine = jnp.sum(
                jnp.where(lane == owned * peer(step), held[...], 0.0), axis=1, keepdims=True
            )
            hit = jnp.where(col == mine, 1.0, 0.0)
            pick[pl.ds(pl.multiple_of(step * cap, cap), cap), :] = hit.astype(bf16)

        at = pl.ds(pl.multiple_of(b * rows_b, rows_b), rows_b)
        rows = jnp.dot(pick[at, :], proj[...], preferred_element_type=f32).astype(bf16)
        qk_s[at, :] = rows[:, : 2 * hd]
        v_s[at, :] = rows[:, 2 * hd :]

    def send_qk(step):
        remote(block(qk_s, step, cap), block(qk_r, me, cap), send_sem.at[1], qk_sem,
               {"seq": peer(step)}).start()

    def send_v(step):
        remote(block(v_s, step, cap), block(v_r, me, cap), send_sem.at[2], v_sem,
               {"seq": peer(step)}).start()

    loads[2].wait()
    loads[3].wait()
    proj[...] = jnp.dot(tokens[...], wqkv[...], preferred_element_type=f32).astype(bf16)
    gather_batch(0)

    pl.semaphore_wait(barrier, n - 1 + heads - 1)

    @pl.loop(1, nz)
    def _(dz):
        remote(cnt_s, tab_r.at[my_x, my_z], send_sem.at[0], cnt_sem.at[0],
               {"seq": lax.rem(my_z + dz, nz) * nx + my_x}).start()

    pltpu.make_async_copy(cnt_s, tab_r.at[my_x, my_z], cnt_sem.at[0]).start()

    @pl.loop(0, batch)
    def _(step):
        send_qk(step)

    @pl.loop(1, batches - 1)
    def _(b):
        gather_batch(b)

        @pl.loop(0, batch)
        def _(i):
            send_qk(b * batch + i)

    gather_batch(batches - 1)

    @pl.loop(own_step + 1, n)
    def _(step):
        send_qk(step)

    pltpu.make_async_copy(block(qk_s, own_step, cap), block(qk_r, me, cap), qk_sem).start()

    column = tab_r.at[my_x]
    pltpu.make_async_copy(column, column, cnt_sem.at[0]).wait()

    @pl.loop(1, nx)
    def _(dx):
        remote(column, column, send_sem.at[6], cnt_sem.at[1],
               {"seq": my_z * nx + lax.rem(my_x + dx, nx)}).start()

    @pl.loop(0, own_step)
    def _(step):
        send_v(step)

    @pl.loop(own_step + 1, n)
    def _(step):
        send_v(step)

    pltpu.make_async_copy(block(v_s, own_step, cap), block(v_r, me, cap), v_sem).start()

    @pl.loop(1, heads)
    def _(step):
        remote(wo, block(all_wo, my_head, hd), send_sem.at[3], wo_sem,
               {"head": lax.rem(my_head + step, heads)}).start()

    pltpu.make_async_copy(wo, block(all_wo, my_head, hd), wo_sem).start()

    for b in range(batches):
        part = pick[b * rows_b : (b + 1) * rows_b, :].astype(f32)
        put[:, b * rows_b : (b + 1) * rows_b] = part.T.astype(bf16)

    others = tab_r.at[pl.ds(0, nx - 1)]
    pltpu.make_async_copy(others, others, cnt_sem.at[1]).wait()

    @pl.loop(0, n)
    def _(s):
        tab[pl.ds(s, 1), :] = tab_r[lax.rem(s, nx), s // nx]

    table = tab[...].astype(bf16)

    def ends(rows_k):
        k_id, c_id = iota((rows_k, clusters), 0), iota((rows_k, clusters), 1)
        inside = (c_id // owned == me) & (lax.rem(c_id, owned) <= k_id)
        return jnp.where(inside, 1.0, 0.0).astype(bf16)

    total_rows = n * cap
    spread_t = jnp.where(iota((n, total_rows), 1) // cap == iota((n, total_rows), 0), 1.0, 0.0)
    end_row = jnp.dot(
        nt_dot(ends(8), table).astype(bf16), spread_t.astype(bf16), preferred_element_type=f32
    )
    past = (lax.rem(iota((8, total_rows), 1), cap).astype(f32) >= end_row) & (
        iota((8, total_rows), 0) < owned
    )
    cl_row = jnp.sum(jnp.where(past, 1.0, 0.0), axis=0, keepdims=True)
    spread = jnp.where(iota((total_rows, n), 0) // cap == iota((total_rows, n), 1), 1.0, 0.0)
    end_col = jnp.dot(
        spread.astype(bf16), nt_dot(table, ends(128)).astype(bf16), preferred_element_type=f32
    )
    past = (lax.rem(iota((total_rows, 128), 0), cap).astype(f32) >= end_col) & (
        iota((total_rows, 128), 1) < owned
    )
    cl_col[...] = jnp.sum(jnp.where(past, 1.0, 0.0), axis=1, keepdims=True)

    pltpu.make_async_copy(qk_r, qk_r, qk_sem).wait()
    scale = hd ** (-0.5)

    @pl.loop(0, total_rows // q_rows)
    def _(c):
        at = pl.ds(pl.multiple_of(c * q_rows, q_rows), q_rows)
        scores = nt_dot(qk_r[at, :hd], qk_r[:, hd:]) * scale
        ahead = iota((q_rows, total_rows), 1) <= iota((q_rows, total_rows), 0) + c * q_rows
        allowed = (cl_col[at, :] == cl_row) & ahead
        masked = jnp.where(allowed, scores, -1e30)
        expo = jnp.exp(masked - jnp.max(masked, axis=1, keepdims=True))
        probs[at, :] = (expo / jnp.sum(expo, axis=1, keepdims=True)).astype(bf16)

    sums = [jnp.zeros((1, hd), f32) for _ in range(owned)]
    keys = qk_r[:, hd:].astype(f32)
    unit = keys * lax.rsqrt(jnp.sum(keys * keys, axis=1, keepdims=True) + eps_norm)
    for k in range(owned):
        kept = jnp.where(cl_col[...] == float(k), unit, 0.0)
        one = jnp.sum(kept, axis=0, keepdims=True)
        cent[k : k + 1, :] = one * lax.rsqrt(jnp.mean(one * one, axis=1, keepdims=True) + eps_norm)

    pltpu.make_async_copy(v_r, v_r, v_sem).wait()

    def batch_of(apart):
        half = pairs // 2
        return jnp.where(apart < half, 2 * (half - apart) - 1, 2 * (apart - half))

    first = batch_of(my_pair)

    @pl.loop(0, batches)
    def _(k):
        b = jnp.where(k == 0, first, jnp.where(k <= first, k - 1, k))
        turn = lax.rem(my_pair + 2 * pairs - offset(b), pairs)
        at = pl.ds(pl.multiple_of(turn * rows_b, rows_b), rows_b)
        o_s[at, :] = jnp.dot(probs[at, :], v_r[...], preferred_element_type=f32).astype(bf16)

        @pl.loop(0, batch)
        def _(i):
            s = turn * batch + i
            step = (
                b * batch
                + lax.rem(my_z + s // nx, 2) * nx
                + lax.rem(my_x - lax.rem(s, nx) + nx, nx)
            )

            @pl.when(s != me)
            def _():
                remote(block(o_s, s, cap), block(o_r, step, cap), send_sem.at[4],
                       o_sem.at[b], {"seq": s}).start()

            @pl.when(s == me)
            def _():
                pltpu.make_async_copy(
                    block(o_s, s, cap), block(o_r, step, cap), o_sem.at[b]
                ).start()

    acc[...] = jnp.zeros_like(acc)
    for b in range(batches):
        at = pl.ds(b * rows_b, rows_b)
        pltpu.make_async_copy(o_r.at[at, :], o_r.at[at, :], o_sem.at[b]).wait()
        acc[...] += jnp.dot(put[:, b * rows_b : (b + 1) * rows_b], o_r[at, :],
                            preferred_element_type=f32)
    hs[...] = acc[...].astype(bf16)
    lanes = all_heads.at[:, pl.ds(pl.multiple_of(my_head * hd, hd), hd)]

    @pl.loop(1, heads)
    def _(step):
        to = lax.rem(my_head + step, heads)
        remote(block(hs, to, out_rows), lanes, send_sem.at[5], h_sem, {"head": to}).start()

    pltpu.make_async_copy(block(hs, my_head, out_rows), lanes, h_sem).start()
    pltpu.make_async_copy(all_wo, all_wo, wo_sem).wait()
    pltpu.make_async_copy(all_heads, all_heads, h_sem).wait()

    def sent(ref, index):
        pltpu.make_async_copy(ref, ref, send_sem.at[index]).wait()

    sent(tab_r.at[0, pl.ds(0, nz - 1)], 0)
    sent(others, 6)
    sent(qk_s.at[pl.ds(0, (n - 1) * cap), :], 1)
    sent(v_s.at[pl.ds(0, (n - 1) * cap), :], 2)
    sent(all_wo.at[pl.ds(0, (heads - 1) * hd), :], 3)
    sent(o_s.at[pl.ds(0, (n - 1) * cap), :], 4)
    sent(hs.at[pl.ds(0, (heads - 1) * out_rows), :], 5)


def mix_kernel(all_heads, all_wo, cent_in, mixed_hbm, cent_hbm, mixed, sems):
    parts = sems.shape[0] - 1
    size = mixed.shape[1] // parts
    copies = [pltpu.make_async_copy(cent_in, cent_hbm, sems.at[parts])]
    copies[0].start()
    for c in range(parts):
        at = pl.ds(c * size, size)
        mixed[:, at] = jnp.dot(
            all_heads[...], all_wo[:, at], preferred_element_type=f32
        ).astype(bf16)
        copies.append(pltpu.make_async_copy(mixed.at[:, at], mixed_hbm.at[:, at], sems.at[c]))
        copies[-1].start()
    for copy in copies:
        copy.wait()


def on_device(nx, tokens, qkv_weight, out_weight, members, counts):
    slab, width = tokens.shape
    heads, n = lax.axis_size("head"), lax.axis_size("seq")
    hd = out_weight.shape[1]
    clusters, s_c = members.shape[1], members.shape[2]
    cap = 2 * slab // n
    rows = n * cap
    batch = 2 * nx
    vm = lambda shape, dtype: pltpu.VMEM(shape, dtype)
    all_heads, all_wo, centroids = pl.pallas_call(
        functools.partial(layer_kernel, nx, batch, 128),
        out_shape=(
            vm((slab // heads, heads * hd), bf16),
            vm((heads * hd, width), bf16),
            vm((clusters // n, hd), f32),
        ),
        in_specs=[pl.BlockSpec(memory_space=pltpu.HBM)] * 5,
        out_specs=(
            pl.BlockSpec(memory_space=pltpu.VMEM),
            pl.BlockSpec(memory_space=pltpu.VMEM),
            pl.BlockSpec(memory_space=pltpu.VMEM),
        ),
        scratch_shapes=[
            vm((slab, width), bf16),
            vm((width, 3 * hd), bf16),
            vm((s_c, 1, clusters), i32),
            vm((1, clusters), i32),
            vm((slab, 3 * hd), bf16),
            vm((rows, slab), bf16),
            vm((slab, rows), bf16),
            vm((rows, 2 * hd), bf16),
            vm((rows, hd), bf16),
            vm((rows, 2 * hd), bf16),
            vm((rows, hd), bf16),
            vm((rows, rows), bf16),
            vm((rows, hd), bf16),
            vm((rows, hd), bf16),
            vm((slab, hd), f32),
            vm((slab, hd), bf16),
            vm((1, clusters), f32),
            vm((nx, n // nx, 1, clusters), f32),
            vm((n, clusters), f32),
            vm((cap, clusters), f32),
            vm((rows, 1), f32),
            pltpu.SemaphoreType.DMA((4,)),
            pltpu.SemaphoreType.DMA((7,)),
            pltpu.SemaphoreType.DMA((2,)),
            pltpu.SemaphoreType.DMA,
            pltpu.SemaphoreType.DMA,
            pltpu.SemaphoreType.DMA((n // batch,)),
            pltpu.SemaphoreType.DMA,
            pltpu.SemaphoreType.DMA,
        ],
        compiler_params=pltpu.CompilerParams(
            collective_id=0, has_side_effects=True, vmem_limit_bytes=44 << 20
        ),
    )(
        *(
            pltpu.with_memory_space_constraint(x, pltpu.HBM)
            for x in (
                tokens,
                qkv_weight.reshape(width, 3 * hd),
                out_weight.reshape(hd, width),
                jnp.transpose(members, (2, 0, 1)),
                counts.reshape(1, clusters),
            )
        )
    )
    parts = 2
    mixed, centroids = pl.pallas_call(
        mix_kernel,
        out_shape=(
            jax.ShapeDtypeStruct((slab // heads, width), bf16),
            jax.ShapeDtypeStruct(centroids.shape, f32),
        ),
        in_specs=[pl.BlockSpec(memory_space=pltpu.VMEM)] * 3,
        out_specs=(pl.BlockSpec(memory_space=pltpu.HBM),) * 2,
        scratch_shapes=[
            vm((slab // heads, width), bf16),
            pltpu.SemaphoreType.DMA((parts + 1,)),
        ],
    )(*(pltpu.with_memory_space_constraint(x, pltpu.VMEM) for x in (all_heads, all_wo, centroids)))
    return mixed, centroids[None]


def solution(mesh):
    n = mesh.shape["seq"]
    return jax.shard_map(
        functools.partial(on_device, min(4, n // 4)),
        mesh=mesh,
        in_specs=(
            P("seq", None),
            P(None, "head", None),
            P("head", None, None),
            P("head", None, "seq"),
            P("head", "seq", None),
        ),
        out_specs=(P(("seq", "head"), None), P("head", "seq", None)),
        check_vma=False,
    )
```

```python
import functools

import jax
import jax.numpy as jnp
from jax import lax
from jax.experimental import pallas as pl
from jax.experimental.pallas import tpu as pltpu
from jax.sharding import PartitionSpec as P

MESH = pl.DeviceIdType.MESH
eps_norm = 1e-06
f32, bf16, i32 = jnp.float32, jnp.bfloat16, jnp.int32


def iota(shape, dim):
    return lax.broadcasted_iota(i32, shape, dim)


def nt_dot(a, b):
    return lax.dot_general(a, b, (((1,), (1,)), ((), ())), preferred_element_type=f32)


def layer_kernel(
    nx, batch, q_rows,
    tokens_hbm, wqkv_hbm, wo, ids_hbm, cnt_hbm,
    all_heads, all_wo, cent,
    tokens, wqkv, ids, cnt, proj, pick, put, qk_s, v_s, qk_r, v_r, probs, o_s, o_r, acc, hs,
    cnt_s, tab_r, tab, held, cl_col,
    in_sem, send_sem, cnt_sem, qk_sem, v_sem, o_sem, h_sem, wo_sem,
):
    n, heads = lax.axis_size("seq"), lax.axis_size("head")
    me, my_head = lax.axis_index("seq"), lax.axis_index("head")
    nz = n // nx
    my_z, my_x = me // nx, lax.rem(me, nx)
    slab, hd = proj.shape[0], wo.shape[0]
    cap = qk_s.shape[0] // n
    clusters = cnt.shape[1]
    pairs = nz // 2
    my_pair, my_odd = my_z // 2, lax.rem(my_z, 2)
    owned = clusters // n
    s_c = ids.shape[0]
    batches = n // batch
    rows_b = batch * cap
    out_rows = all_heads.shape[0]

    def offset(b):
        return pairs // 2 + (b + 1) // 2 * (1 - 2 * lax.rem(b, 2))

    own_step = (batches - 1) * batch

    def peer(step):
        b, i = step // batch, lax.rem(step, batch)
        pair = lax.rem(my_pair + offset(b), pairs)
        return (pair * 2 + lax.rem(my_odd + i // nx, 2)) * nx + lax.rem(my_x + i, nx)

    def block(ref, index, size):
        return ref.at[pl.ds(pl.multiple_of(index * size, size), size), :]

    def remote(src, dst, ssem, rsem, where):
        return pltpu.make_async_remote_copy(
            src_ref=src, dst_ref=dst, send_sem=ssem, recv_sem=rsem,
            device_id=where, device_id_type=MESH,
        )

    loads = [
        pltpu.make_async_copy(ids_hbm, ids, in_sem.at[0]),
        pltpu.make_async_copy(cnt_hbm, cnt, in_sem.at[1]),
        pltpu.make_async_copy(wqkv_hbm, wqkv, in_sem.at[2]),
        pltpu.make_async_copy(tokens_hbm, tokens, in_sem.at[3]),
    ]
    for load in loads:
        load.start()

    barrier = pltpu.get_barrier_semaphore()

    @pl.loop(1, n)
    def _(step):
        pl.semaphore_signal(
            barrier, inc=1, device_id={"seq": lax.rem(me + step, n)}, device_id_type=MESH
        )

    @pl.loop(1, heads)
    def _(step):
        pl.semaphore_signal(
            barrier, inc=1, device_id={"head": lax.rem(my_head + step, heads)}, device_id_type=MESH
        )

    loads[0].wait()
    loads[1].wait()
    local = jnp.concatenate([ids[j] for j in range(s_c)], axis=0) - me * slab
    count = cnt[...]
    rank = jnp.zeros((s_c, clusters), i32)
    for j in range(s_c):
        rank += jnp.where((local[j : j + 1, :] < local) & (count > j), 1, 0)
    wide = jnp.broadcast_to(count, (8, clusters))
    lane4 = lax.rem(iota((8, clusters), 1), owned)
    start = jnp.zeros((8, clusters), i32)
    for k in range(1, owned):
        start += jnp.where(lane4 >= k, pltpu.roll(wide, k, 1), 0)
    slot = jnp.where(iota((s_c, clusters), 0) < count, rank + start[:1, :], -1)
    token = jnp.zeros((cap, clusters), f32)
    row = iota((cap, clusters), 0)
    for j in range(s_c):
        token += jnp.where(slot[j : j + 1, :] == row, (local[j : j + 1, :] + 1).astype(f32), 0.0)
    total = token
    for k in range(1, owned):
        total += pltpu.roll(token, clusters - k, 1)
    held[...] = total
    cnt_s[...] = count.astype(f32)

    col = (iota((cap, slab), 1) + 1).astype(f32)
    lane = iota((cap, clusters), 1)

    def gather_batch(b):
        for i in range(batch):
            step = b * batch + i
            mine = jnp.sum(
                jnp.where(lane == owned * peer(step), held[...], 0.0), axis=1, keepdims=True
            )
            hit = jnp.where(col == mine, 1.0, 0.0)
            pick[pl.ds(pl.multiple_of(step * cap, cap), cap), :] = hit.astype(bf16)

        at = pl.ds(pl.multiple_of(b * rows_b, rows_b), rows_b)
        rows = jnp.dot(pick[at, :], proj[...], preferred_element_type=f32).astype(bf16)
        qk_s[at, :] = rows[:, : 2 * hd]
        v_s[at, :] = rows[:, 2 * hd :]

    def send_qk(step):
        remote(block(qk_s, step, cap), block(qk_r, me, cap), send_sem.at[1], qk_sem,
               {"seq": peer(step)}).start()

    def send_v(step):
        remote(block(v_s, step, cap), block(v_r, me, cap), send_sem.at[2], v_sem,
               {"seq": peer(step)}).start()

    loads[2].wait()
    loads[3].wait()
    proj[...] = jnp.dot(tokens[...], wqkv[...], preferred_element_type=f32).astype(bf16)
    gather_batch(0)

    pl.semaphore_wait(barrier, n - 1 + heads - 1)

    @pl.loop(1, nz)
    def _(dz):
        remote(cnt_s, tab_r.at[my_x, my_z], send_sem.at[0], cnt_sem.at[0],
               {"seq": lax.rem(my_z + dz, nz) * nx + my_x}).start()

    pltpu.make_async_copy(cnt_s, tab_r.at[my_x, my_z], cnt_sem.at[0]).start()

    @pl.loop(0, batch)
    def _(step):
        send_qk(step)

    @pl.loop(1, batches - 1)
    def _(b):
        gather_batch(b)

        @pl.loop(0, batch)
        def _(i):
            send_qk(b * batch + i)

    gather_batch(batches - 1)

    @pl.loop(own_step + 1, n)
    def _(step):
        send_qk(step)

    pltpu.make_async_copy(block(qk_s, own_step, cap), block(qk_r, me, cap), qk_sem).start()

    column = tab_r.at[my_x]
    pltpu.make_async_copy(column, column, cnt_sem.at[0]).wait()

    @pl.loop(1, nx)
    def _(dx):
        remote(column, column, send_sem.at[6], cnt_sem.at[1],
               {"seq": my_z * nx + lax.rem(my_x + dx, nx)}).start()

    @pl.loop(0, own_step)
    def _(step):
        send_v(step)

    @pl.loop(own_step + 1, n)
    def _(step):
        send_v(step)

    pltpu.make_async_copy(block(v_s, own_step, cap), block(v_r, me, cap), v_sem).start()

    @pl.loop(1, heads)
    def _(step):
        remote(wo, block(all_wo, my_head, hd), send_sem.at[3], wo_sem,
               {"head": lax.rem(my_head + step, heads)}).start()

    pltpu.make_async_copy(wo, block(all_wo, my_head, hd), wo_sem).start()

    for b in range(batches):
        part = pick[b * rows_b : (b + 1) * rows_b, :].astype(f32)
        put[:, b * rows_b : (b + 1) * rows_b] = part.T.astype(bf16)

    others = tab_r.at[pl.ds(0, nx - 1)]
    pltpu.make_async_copy(others, others, cnt_sem.at[1]).wait()

    @pl.loop(0, n)
    def _(s):
        tab[pl.ds(s, 1), :] = tab_r[lax.rem(s, nx), s // nx]

    table = tab[...].astype(bf16)

    def ends(rows_k):
        k_id, c_id = iota((rows_k, clusters), 0), iota((rows_k, clusters), 1)
        inside = (c_id // owned == me) & (lax.rem(c_id, owned) <= k_id)
        return jnp.where(inside, 1.0, 0.0).astype(bf16)

    total_rows = n * cap
    spread_t = jnp.where(iota((n, total_rows), 1) // cap == iota((n, total_rows), 0), 1.0, 0.0)
    end_row = jnp.dot(
        nt_dot(ends(8), table).astype(bf16), spread_t.astype(bf16), preferred_element_type=f32
    )
    past = (lax.rem(iota((8, total_rows), 1), cap).astype(f32) >= end_row) & (
        iota((8, total_rows), 0) < owned
    )
    cl_row = jnp.sum(jnp.where(past, 1.0, 0.0), axis=0, keepdims=True)
    spread = jnp.where(iota((total_rows, n), 0) // cap == iota((total_rows, n), 1), 1.0, 0.0)
    end_col = jnp.dot(
        spread.astype(bf16), nt_dot(table, ends(128)).astype(bf16), preferred_element_type=f32
    )
    past = (lax.rem(iota((total_rows, 128), 0), cap).astype(f32) >= end_col) & (
        iota((total_rows, 128), 1) < owned
    )
    cl_col[...] = jnp.sum(jnp.where(past, 1.0, 0.0), axis=1, keepdims=True)

    pltpu.make_async_copy(qk_r, qk_r, qk_sem).wait()
    scale = hd ** (-0.5)

    @pl.loop(0, total_rows // q_rows)
    def _(c):
        at = pl.ds(pl.multiple_of(c * q_rows, q_rows), q_rows)
        scores = nt_dot(qk_r[at, :hd], qk_r[:, hd:]) * scale
        ahead = iota((q_rows, total_rows), 1) <= iota((q_rows, total_rows), 0) + c * q_rows
        allowed = (cl_col[at, :] == cl_row) & ahead
        masked = jnp.where(allowed, scores, -1e30)
        expo = jnp.exp(masked - jnp.max(masked, axis=1, keepdims=True))
        probs[at, :] = (expo / jnp.sum(expo, axis=1, keepdims=True)).astype(bf16)

    sums = [jnp.zeros((1, hd), f32) for _ in range(owned)]
    keys = qk_r[:, hd:].astype(f32)
    unit = keys * lax.rsqrt(jnp.sum(keys * keys, axis=1, keepdims=True) + eps_norm)
    for k in range(owned):
        kept = jnp.where(cl_col[...] == float(k), unit, 0.0)
        one = jnp.sum(kept, axis=0, keepdims=True)
        cent[k : k + 1, :] = one * lax.rsqrt(jnp.mean(one * one, axis=1, keepdims=True) + eps_norm)

    pltpu.make_async_copy(v_r, v_r, v_sem).wait()

    def batch_of(apart):
        half = pairs // 2
        return jnp.where(apart < half, 2 * (half - apart) - 1, 2 * (apart - half))

    first = batch_of(my_pair)

    @pl.loop(0, batches)
    def _(k):
        b = jnp.where(k == 0, first, jnp.where(k <= first, k - 1, k))
        turn = lax.rem(my_pair + 2 * pairs - offset(b), pairs)
        at = pl.ds(pl.multiple_of(turn * rows_b, rows_b), rows_b)
        o_s[at, :] = jnp.dot(probs[at, :], v_r[...], preferred_element_type=f32).astype(bf16)

        @pl.loop(0, batch)
        def _(i):
            s = turn * batch + i
            step = (
                b * batch
                + lax.rem(my_z + s // nx, 2) * nx
                + lax.rem(my_x - lax.rem(s, nx) + nx, nx)
            )

            @pl.when(s != me)
            def _():
                remote(block(o_s, s, cap), block(o_r, step, cap), send_sem.at[4],
                       o_sem.at[b], {"seq": s}).start()

            @pl.when(s == me)
            def _():
                pltpu.make_async_copy(
                    block(o_s, s, cap), block(o_r, step, cap), o_sem.at[b]
                ).start()

    acc[...] = jnp.zeros_like(acc)

    def returned(b):
        at = pl.ds(b * rows_b, rows_b)
        pltpu.make_async_copy(o_r.at[at, :], o_r.at[at, :], o_sem.at[b]).wait()
        return at

    for b in range(batches - 1):
        at = returned(b)
        acc[...] += jnp.dot(put[:, at], o_r[at, :], preferred_element_type=f32)

    at = returned(batches - 1)
    lanes = all_heads.at[:, pl.ds(pl.multiple_of(my_head * hd, hd), hd)]

    def finish(to):
        tokens_at = pl.ds(pl.multiple_of(to * out_rows, out_rows), out_rows)
        rest = jnp.dot(put[tokens_at, at], o_r[at, :], preferred_element_type=f32)
        hs[tokens_at, :] = (acc[tokens_at, :] + rest).astype(bf16)

    for step in range(1, heads):
        to = lax.rem(my_head + step, heads)
        finish(to)
        remote(block(hs, to, out_rows), lanes, send_sem.at[5], h_sem, {"head": to}).start()

    finish(my_head)
    pltpu.make_async_copy(block(hs, my_head, out_rows), lanes, h_sem).start()
    pltpu.make_async_copy(all_wo, all_wo, wo_sem).wait()
    pltpu.make_async_copy(all_heads, all_heads, h_sem).wait()

    def sent(ref, index):
        pltpu.make_async_copy(ref, ref, send_sem.at[index]).wait()

    sent(tab_r.at[0, pl.ds(0, nz - 1)], 0)
    sent(others, 6)
    sent(qk_s.at[pl.ds(0, (n - 1) * cap), :], 1)
    sent(v_s.at[pl.ds(0, (n - 1) * cap), :], 2)
    sent(all_wo.at[pl.ds(0, (heads - 1) * hd), :], 3)
    sent(o_s.at[pl.ds(0, (n - 1) * cap), :], 4)
    sent(hs.at[pl.ds(0, (heads - 1) * out_rows), :], 5)


def mix_kernel(all_heads, all_wo, cent_in, mixed_hbm, cent_hbm, mixed, sems):
    parts = sems.shape[0] - 1
    size = mixed.shape[1] // parts
    copies = [pltpu.make_async_copy(cent_in, cent_hbm, sems.at[parts])]
    copies[0].start()
    for c in range(parts):
        at = pl.ds(c * size, size)
        mixed[:, at] = jnp.dot(
            all_heads[...], all_wo[:, at], preferred_element_type=f32
        ).astype(bf16)
        copies.append(pltpu.make_async_copy(mixed.at[:, at], mixed_hbm.at[:, at], sems.at[c]))
        copies[-1].start()
    for copy in copies:
        copy.wait()


def on_device(nx, tokens, qkv_weight, out_weight, members, counts):
    slab, width = tokens.shape
    heads, n = lax.axis_size("head"), lax.axis_size("seq")
    hd = out_weight.shape[1]
    clusters, s_c = members.shape[1], members.shape[2]
    cap = 2 * slab // n
    rows = n * cap
    batch = 2 * nx
    vm = lambda shape, dtype: pltpu.VMEM(shape, dtype)
    all_heads, all_wo, centroids = pl.pallas_call(
        functools.partial(layer_kernel, nx, batch, 128),
        out_shape=(
            vm((slab // heads, heads * hd), bf16),
            vm((heads * hd, width), bf16),
            vm((clusters // n, hd), f32),
        ),
        in_specs=[pl.BlockSpec(memory_space=pltpu.HBM)] * 5,
        out_specs=(
            pl.BlockSpec(memory_space=pltpu.VMEM),
            pl.BlockSpec(memory_space=pltpu.VMEM),
            pl.BlockSpec(memory_space=pltpu.VMEM),
        ),
        scratch_shapes=[
            vm((slab, width), bf16),
            vm((width, 3 * hd), bf16),
            vm((s_c, 1, clusters), i32),
            vm((1, clusters), i32),
            vm((slab, 3 * hd), bf16),
            vm((rows, slab), bf16),
            vm((slab, rows), bf16),
            vm((rows, 2 * hd), bf16),
            vm((rows, hd), bf16),
            vm((rows, 2 * hd), bf16),
            vm((rows, hd), bf16),
            vm((rows, rows), bf16),
            vm((rows, hd), bf16),
            vm((rows, hd), bf16),
            vm((slab, hd), f32),
            vm((slab, hd), bf16),
            vm((1, clusters), f32),
            vm((nx, n // nx, 1, clusters), f32),
            vm((n, clusters), f32),
            vm((cap, clusters), f32),
            vm((rows, 1), f32),
            pltpu.SemaphoreType.DMA((4,)),
            pltpu.SemaphoreType.DMA((7,)),
            pltpu.SemaphoreType.DMA((2,)),
            pltpu.SemaphoreType.DMA,
            pltpu.SemaphoreType.DMA,
            pltpu.SemaphoreType.DMA((n // batch,)),
            pltpu.SemaphoreType.DMA,
            pltpu.SemaphoreType.DMA,
        ],
        compiler_params=pltpu.CompilerParams(
            collective_id=0, has_side_effects=True, vmem_limit_bytes=44 << 20
        ),
    )(
        *(
            pltpu.with_memory_space_constraint(x, pltpu.HBM)
            for x in (
                tokens,
                qkv_weight.reshape(width, 3 * hd),
                out_weight.reshape(hd, width),
                jnp.transpose(members, (2, 0, 1)),
                counts.reshape(1, clusters),
            )
        )
    )
    parts = 2
    mixed, centroids = pl.pallas_call(
        mix_kernel,
        out_shape=(
            jax.ShapeDtypeStruct((slab // heads, width), bf16),
            jax.ShapeDtypeStruct(centroids.shape, f32),
        ),
        in_specs=[pl.BlockSpec(memory_space=pltpu.VMEM)] * 3,
        out_specs=(pl.BlockSpec(memory_space=pltpu.HBM),) * 2,
        scratch_shapes=[
            vm((slab // heads, width), bf16),
            pltpu.SemaphoreType.DMA((parts + 1,)),
        ],
    )(*(pltpu.with_memory_space_constraint(x, pltpu.VMEM) for x in (all_heads, all_wo, centroids)))
    return mixed, centroids[None]


def solution(mesh):
    n = mesh.shape["seq"]
    return jax.shard_map(
        functools.partial(on_device, min(4, n // 4)),
        mesh=mesh,
        in_specs=(
            P("seq", None),
            P(None, "head", None),
            P("head", None, None),
            P("head", None, "seq"),
            P("head", "seq", None),
        ),
        out_specs=(P(("seq", "head"), None), P("head", "seq", None)),
        check_vma=False,
    )
```
